32 devices in a mesh: patch: 2 (over x), epoch: 16 (over z, y, core).
Axes of the slice: x: 2, y: 2, z: 4, core: 2. Of those that a mesh axis runs over, the one named last changes fastest.
Arguments:
- images: float32 [32, 128, 1024], P(('patch', 'epoch')), parts along dimension 0, may hold values from -20 to 20, as said below
- variance: float32 [32], P(('patch', 'epoch')), parts along dimension 0, may hold values from 0.25 to 4
- zero_point: float32 [32], P(('patch', 'epoch')), parts along dimension 0, may hold values from 0.5 to 2
- block_mask: int32 [32, 1], P(('patch', 'epoch')), parts along dimension 0, may hold values 0 or 1
- stamps: int32 [32, 512], P(('patch', 'epoch')), parts along dimension 0, may hold values from 0 to 131071
- owners: int32 [8], P('patch'), parts along dimension 0, may hold values from 0 to 15
Outputs:
- significance: float32 [32, 128, 1024], P(('patch', 'epoch')), parts along dimension 0
- coefficients: float32 [32, 15], P(('patch', 'epoch')), parts along dimension 0
The draws below stay inside these ranges and needn't reach their ends.
There are 2 independent parts, one for each index of `patch`. The reference program is written for one: setup_inputs(seed, part) draws one part's arguments, and reference() takes and returns one part's arrays. A program takes and returns all parts, laid end to end along the dimension named above; each array names one. Nothing has to cross between parts.
Inputs may be any that keep to these rules, and one draw needn't show every extreme that they name: `images`: each epoch is a common sky times an epoch scale plus noise.
All inputs are finite; a program needn't handle non-finite values. No bound on the sum of `block_mask` on one device may be relied on, other than what follows from the above.
Results may differ from the reference program's by a relative error of at most 0.00075.
The reference program's roundings to bfloat16 on the way count: a program that leaves them out, or rounds other values in their place, can miss the bound.
Values sent between devices are 32-bit elements; how exact they have to be, the bound alone decides.
A program may use at most 64 MiB of HBM per device.

```python
import math
import jax
import jax.numpy as jnp
from jax import lax

H = 128
W = 1024
TILES = 4
KHALF = 7
NBASIS = 12
NSTAMP = 512
NBLOCK = 1
EPOCHS = 16


def draw_images(key, part):
    sky = jnp.clip(jax.random.normal(jax.random.fold_in(key, 11), (H, W), jnp.float32), -6.0, 6.0)
    scales = jax.random.uniform(jax.random.fold_in(key, 12), (EPOCHS,), jnp.float32, 0.5, 1.5)
    noise = 0.3 * jnp.clip(jax.random.normal(jax.random.fold_in(key, 14), (EPOCHS, H, W), jnp.float32), -6.0, 6.0)
    return scales[:, None, None] * sky[None] + noise


def with_ends(drawn, stream_key, least, high):
    longest = drawn.shape.index(max(drawn.shape))
    spots = []
    for shift in (0, 1):
        where = [jax.random.randint(jax.random.fold_in(stream_key, axis), (), 0, length) for axis, length in enumerate(drawn.shape)]
        where[longest] = (where[longest] + shift) % drawn.shape[longest]
        spots.append(tuple(where))
    return drawn.at[spots[0]].set(least).at[spots[1]].set(high)


def block_levels(own_key, dims, pieces, smallest, top_value):
    factor_of, own = 1.0, jax.random.fold_in(own_key, 6)
    for dim, blocks in pieces:
        heights = jnp.exp(jax.random.uniform(jax.random.fold_in(own, dim), (blocks,), jnp.float32, smallest / len(pieces), top_value / len(pieces)))
        factor_of = factor_of * jnp.repeat(heights, dims[dim] // blocks).reshape([-1 if axis == dim else 1 for axis in range(len(dims))])
    return factor_of


def setup_inputs(seed: int = 0, part: int = 0) -> dict:
    seeds = jax.random.split(jax.random.key(seed), 7)
    part_splits = jax.random.split(jax.random.fold_in(seeds[6], part), 7)
    images = draw_images(jax.random.fold_in(jax.random.fold_in(seeds[6], part), 71), part)
    variance = jnp.clip(jnp.exp(math.log(4.0) - 2.7725887 * jax.random.uniform(part_splits[1], (EPOCHS,), jnp.float32) ** block_levels(part_splits[1], (EPOCHS,), ((0, 16),), -0.2, 0.2)), 0.25, 4.0)
    zero_point = jnp.clip(jnp.exp(math.log(2.0) - 1.3862944 * jax.random.uniform(part_splits[2], (EPOCHS,), jnp.float32) ** block_levels(part_splits[2], (EPOCHS,), ((0, 16),), -0.2, 0.2)), 0.5, 2.0)
    block_mask = with_ends((jax.random.randint(part_splits[3], (EPOCHS, NBLOCK), 0, 4) < 3).astype(jnp.int32), jax.random.fold_in(part_splits[3], 1), 0, 1)
    stamps = with_ends(jax.random.randint(part_splits[4], (EPOCHS, NSTAMP), 0, H * W), jax.random.fold_in(part_splits[4], 1), 0, (H * W) - 1).astype(jnp.int32)
    owners = with_ends(jax.random.randint(part_splits[5], (TILES,), 0, EPOCHS), jax.random.fold_in(part_splits[5], 1), 0, EPOCHS - 1).astype(jnp.int32)
    return {"images": images, "variance": variance, "zero_point": zero_point, "block_mask": block_mask, "stamps": stamps, "owners": owners}


sigma_list = (0.75, 1.5, 3.0)
basis_pairs = ((0, 0), (2, 0), (0, 2), (1, 1))

def raise_power(scaled, degree):
    result = jnp.ones_like(scaled)
    for step in range(degree):
        result = result * scaled
    return result

def tap_values(offset, sigma, degree):
    scaled = offset / sigma
    value = jnp.exp(-0.5 * scaled * scaled) * raise_power(scaled, degree) / (math.sqrt(2.0 * math.pi) * sigma)
    value = jnp.where(jnp.abs(offset) <= KHALF, value, 0.0)
    return value.astype(jnp.bfloat16)

def tap_vector(sigma, degree):
    offset = jnp.arange(-KHALF, KHALF + 1).astype(jnp.float32)
    return tap_values(offset, sigma, degree).astype(jnp.float32)

def correlate_cols(field, taps):
    padded = jnp.pad(field, ((0, 0), (KHALF, KHALF)))
    total = jnp.zeros(field.shape, jnp.float32)
    for shift in range(2 * KHALF + 1):
        total = total + taps[shift] * padded[:, shift:shift + field.shape[1]]
    return total

def correlate_rows(field, taps):
    padded = jnp.pad(field, ((KHALF, KHALF), (0, 0)))
    total = jnp.zeros(field.shape, jnp.float32)
    for shift in range(2 * KHALF + 1):
        total = total + taps[shift] * padded[shift:shift + field.shape[0], :]
    return total

def one_epoch(image, stamp_row, mask_row, reference_img):
    sharp = lax.optimization_barrier(image.astype(jnp.bfloat16)).astype(jnp.float32)
    bases = []
    for sigma in sigma_list:
        across = {}
        for degree in (0, 1, 2):
            temp = correlate_cols(sharp, tap_vector(sigma, degree)).astype(jnp.bfloat16)
            across[degree] = lax.optimization_barrier(temp).astype(jnp.float32)
        for pair in basis_pairs:
            bases.append(correlate_rows(across[pair[0]], tap_vector(sigma, pair[1])).astype(jnp.bfloat16))
    xn = 2.0 * (jnp.arange(W).astype(jnp.float32) + 0.5) / W - 1.0
    yn = 2.0 * (jnp.arange(H).astype(jnp.float32) + 0.5) / H - 1.0
    cols = stamp_row % W
    rows = stamp_row // W
    picks = [jnp.take(b.reshape(-1), stamp_row).astype(jnp.float32) for b in bases]
    picks = picks + [jnp.ones((NSTAMP,), jnp.float32), xn[cols], yn[rows]]
    design = jnp.stack(picks, axis=0)
    normal = jnp.dot(design, design.T, precision=lax.Precision.HIGHEST)
    normal = normal + 0.05 * jnp.diag(jnp.diag(normal))
    rhs = jnp.dot(design, jnp.take(reference_img.reshape(-1), stamp_row), precision=lax.Precision.HIGHEST)
    factor = jnp.linalg.cholesky(normal)
    coef = jax.scipy.linalg.cho_solve((factor, True), rhs)
    model = jnp.zeros((H, W), jnp.float32)
    for index in range(NBASIS):
        model = model + coef[index] * bases[index].astype(jnp.float32)
    model = model + coef[NBASIS] + coef[NBASIS + 1] * xn[None, :] + coef[NBASIS + 2] * yn[:, None]
    pixel_mask = jnp.repeat(mask_row.astype(jnp.float32), 128)
    diff = pixel_mask[:, None] * (model - reference_img)
    return (diff, coef)

def reference(images, variance, zero_point, block_mask, stamps, owners):
    weight = 1.0 / variance
    block_w = weight[:, None] * block_mask.astype(jnp.float32)
    row_w = jnp.repeat(block_w, 128, axis=1)
    numerator = jnp.einsum('ey,eyx->yx', row_w, images, precision=lax.Precision.HIGHEST)
    denominator = 1.0 + lax.optimization_barrier(jnp.sum(block_w, axis=0))
    owner_scale = lax.optimization_barrier(jnp.sum((owners[:, None] == jnp.arange(EPOCHS)[None, :]).astype(jnp.float32) * zero_point[None, :], axis=1))
    col_scale = jnp.repeat(owner_scale, W // TILES)
    den_rows = jnp.repeat(denominator, 128)
    reference_img = numerator / den_rows[:, None] * col_scale[None, :]
    diffs, coefs = lax.map(lambda item: one_epoch(item[0], item[1], item[2], reference_img), (images, stamps, block_mask))
    pooled = lax.optimization_barrier(jnp.sum(diffs * diffs, axis=0))
    scatter = jnp.sqrt(0.05 + pooled / EPOCHS)
    return (diffs / scatter[None], coefs)
```

```python
import functools
import math

import jax
import jax.numpy as jnp
from jax import lax
from jax.experimental import pallas as pl
from jax.experimental.pallas import tpu as pltpu
from jax.sharding import PartitionSpec as P

TILES = 4
KHALF = 7
NBASIS = 12
CHUNKS = 2
LANES = 128

sigma_list = (0.75, 1.5, 3.0)
basis_pairs = ((0, 0), (2, 0), (0, 2), (1, 1))
MESH = pl.DeviceIdType.MESH


def tap_values(offset, sigma, degree):
    scaled = offset / sigma
    power = jnp.ones_like(scaled)
    for _ in range(degree):
        power = power * scaled
    value = jnp.exp(-0.5 * scaled * scaled) * power / (math.sqrt(2.0 * math.pi) * sigma)
    return jnp.where(jnp.abs(offset) <= KHALF, value, 0.0).astype(jnp.bfloat16)


def grid_of(count):
    chips = count // 2
    middle = 1
    while middle * 2 * middle * 2 <= chips:
        middle *= 2
    if chips % middle:
        middle = 1
    return chips // middle, middle


def kernel(
    count, height, width,
    image_ref, var_ref, zp_ref, mask_ref, owner_ref, stamp_ref,
    out_ref, coef_ref,
    x1, x2, g1, g2, ra1, ra2, rb1, rb2, rc1, rc2,
    s_own, s_mid, s_sum, sa, sb, sc,
    lhs, across, bases, onehot, design, diff_s,
    send1, recv1, send2, recv2, send3, recv3,
):
    zn, yn_count = grid_of(count)
    half = zn * yn_count
    chunks, _, pr, pcc = x1.shape
    subs = width // chunks // pcc
    groups = height // pr
    cw = width // chunks
    npix = stamp_ref.shape[1]

    me = lax.axis_index("epoch")
    core = lax.rem(me, 2)
    chip = me // 2
    y = lax.rem(chip, yn_count)
    z = chip // yn_count

    def device(zz, yy, cc):
        return {"epoch": (zz * yn_count + yy) * 2 + cc}

    mate = device(z, y, 1 - core)
    ys = [lax.rem(y + d, yn_count) for d in range(1, yn_count)]
    zs = [lax.rem(z + d, zn) for d in range(1, zn)]
    peers = [mate] + [device(z, yy, core) for yy in ys] + [device(zz, y, core) for zz in zs]
    mine = (core * yn_count + y) * zn + z

    barrier = pltpu.get_barrier_semaphore()
    for peer in peers:
        pl.semaphore_signal(barrier, inc=1, device_id=peer, device_id_type=MESH)

    pending = []

    class Lane:
        def __init__(self, send, recv):
            self.send, self.recv, self.next = send, recv, 0

        def start(self, src, dst, device_id):
            copy = pltpu.make_async_remote_copy(
                src_ref=src, dst_ref=dst, send_sem=self.send.at[self.next], recv_sem=self.recv.at[self.next],
                device_id=device_id, device_id_type=MESH,
            )
            self.next += 1
            copy.start()
            pending.append(copy)
            return copy

    class Reduce:
        def __init__(self, x, g, ra, rb, rc, lane):
            self.x, self.g, self.ra, self.rb, self.rc, self.lane = x, g, ra, rb, rc, lane
            self.at = {}

        def a(self, ch):
            self.at["a", ch] = [
                self.lane.start(self.x.at[ch, pl.ds((1 - core) * half, half)], self.ra.at[ch], mate)
            ]

        def wait(self, stage, ch):
            for copy in self.at[stage, ch]:
                copy.wait_recv()

        def b(self, ch):
            self.wait("a", ch)
            for i in range(half):
                self.x[ch, core * half + i] = self.x[ch, core * half + i] + self.ra[ch, i]
            self.at["b", ch] = [
                self.lane.start(
                    self.x.at[ch, pl.ds(core * half + yy * zn, zn)], self.rb.at[ch, d], device(z, yy, core)
                )
                for d, yy in enumerate(ys)
            ]

        def c(self, ch):
            self.wait("b", ch)
            base = core * half + y * zn
            for i in range(zn):
                total = self.x[ch, base + i]
                for d in range(yn_count - 1):
                    total = total + self.rb[ch, d, i]
                self.x[ch, base + i] = total
            self.at["c", ch] = [
                self.lane.start(self.x.at[ch, base + zz], self.rc.at[ch, d], device(zz, y, core))
                for d, zz in enumerate(zs)
            ]

        def d(self, ch, final):
            self.wait("c", ch)
            total = self.x[ch, mine]
            for d in range(zn - 1):
                total = total + self.rc[ch, d]
            self.g[ch, mine] = final(ch, total)
            self.at["d", ch] = [
                self.lane.start(self.g.at[ch, mine], self.g.at[ch, mine], device(zz, y, core)) for zz in zs
            ]

        def e(self, ch):
            self.wait("d", ch)
            block = self.g.at[ch, pl.ds((core * yn_count + y) * zn, zn)]
            self.at["e", ch] = [self.lane.start(block, block, device(z, yy, core)) for yy in ys]

        def f(self, ch):
            self.wait("e", ch)
            block = self.g.at[ch, pl.ds(core * half, half)]
            self.at["f", ch] = [self.lane.start(block, block, mate)]

        def h(self, ch):
            self.wait("f", ch)

    def group(ref, ch, gi):
        parts = [ref[ch, gi * subs + s] for s in range(subs)]
        return parts[0] if subs == 1 else jnp.concatenate(parts, axis=1)

    def put_group(ref, ch, gi, value):
        for s in range(subs):
            ref[ch, gi * subs + s] = value[:, s * pcc:(s + 1) * pcc]

    one = Reduce(x1, g1, ra1, rb1, rc1, Lane(send1, recv1))
    two = Reduce(x2, g2, ra2, rb2, rc2, Lane(send2, recv2))
    tiny = Lane(send3, recv3)

    weight = 1.0 / jnp.full((8, LANES), var_ref[0], jnp.float32)
    mask = jnp.full((8, LANES), mask_ref[0, 0].astype(jnp.float32), jnp.float32)
    block_term = weight * mask
    term = block_term[0:1, 0:1]
    lane = lax.broadcasted_iota(jnp.int32, (8, LANES), 1)
    small = jnp.where(lane == TILES, block_term, 0.0)
    for t in range(TILES):
        value = jnp.where(owner_ref[t] == me, zp_ref[0], 0.0)
        small = small + jnp.where(lane == t, value, 0.0)
    s_own[...] = small
    for ch in range(chunks):
        for gi in range(groups):
            put_group(x1, ch, gi, image_ref[0, gi * pr:(gi + 1) * pr, ch * cw:(ch + 1) * cw] * term)

    pl.semaphore_wait(barrier, len(peers))
    tiny_a = [tiny.start(s_own, sa, mate)]
    for ch in range(chunks):
        one.a(ch)

    sharp = image_ref[0].astype(jnp.bfloat16)
    ntile = width // LANES
    zero = jnp.zeros((height, LANES), jnp.bfloat16)
    for t in range(ntile):
        for s in range(3):
            src = t + s - 1
            value = sharp[:, src * LANES:(src + 1) * LANES] if 0 <= src < ntile else zero
            lhs[t * height:(t + 1) * height, s * LANES:(s + 1) * LANES] = value
    off_h = (
        lax.broadcasted_iota(jnp.int32, (3 * LANES, LANES), 0)
        - LANES
        - lax.broadcasted_iota(jnp.int32, (3 * LANES, LANES), 1)
    ).astype(jnp.float32)
    off_v = (
        lax.broadcasted_iota(jnp.int32, (height, height), 1) - lax.broadcasted_iota(jnp.int32, (height, height), 0)
    ).astype(jnp.float32)

    def horizontal(si):
        sigma = sigma_list[si]
        band = jnp.concatenate([tap_values(off_h, sigma, degree) for degree in (0, 1, 2)], axis=1)
        for t in range(0, ntile, 2):
            res = jnp.dot(
                lhs[t * height:(t + 2) * height, :], band, preferred_element_type=jnp.float32
            ).astype(jnp.bfloat16)
            for u in range(2):
                for degree in (0, 1, 2):
                    across[si * 3 + degree, :, (t + u) * LANES:(t + u + 1) * LANES] = res[
                        u * height:(u + 1) * height, degree * LANES:(degree + 1) * LANES
                    ]

    def vertical(si):
        sigma = sigma_list[si]
        bands = [tap_values(off_v, sigma, degree) for degree in (0, 1, 2)]
        for i, j in basis_pairs:
            k = si * 4 + basis_pairs.index((i, j))
            bases[k * height:(k + 1) * height, :] = jnp.dot(
                bands[j], across[si * 3 + i], preferred_element_type=jnp.float32
            ).astype(jnp.bfloat16)

    for si in range(3):
        horizontal(si)

    tiny_a[0].wait_recv()
    s_mid[...] = s_own[...] + sa[...]
    tiny_b = [tiny.start(s_mid, sb.at[d], device(z, yy, core)) for d, yy in enumerate(ys)]
    for ch in range(chunks):
        one.b(ch)

    for si in range(3):
        vertical(si)

    for copy in tiny_b:
        copy.wait_recv()
    total = s_mid[...]
    for d in range(yn_count - 1):
        total = total + sb[d]
    s_sum[...] = total
    tiny_c = [tiny.start(s_sum, sc.at[d], device(zz, y, core)) for d, zz in enumerate(zs)]
    for ch in range(chunks):
        one.c(ch)

    stamp = stamp_ref[...]
    shift = width.bit_length() - 1
    rows = lax.shift_right_logical(stamp, shift)
    cols = stamp - lax.shift_left(rows, shift)
    onehot[...] = jnp.where(
        lax.broadcasted_iota(jnp.int32, (width, npix), 0) == cols, 1.0, 0.0
    ).astype(jnp.bfloat16)
    row_hit = lax.broadcasted_iota(jnp.int32, (height, npix), 0) == rows
    design[...] = jnp.zeros_like(design)

    def pick(k):
        got = jnp.dot(
            bases[k * height:(k + 1) * height, :], onehot[...], preferred_element_type=jnp.float32
        )
        design[16 + k:17 + k, :] = jnp.sum(jnp.where(row_hit, got, 0.0), axis=0, keepdims=True)

    for k in range(NBASIS):
        pick(k)
    design[16 + NBASIS:17 + NBASIS, :] = jnp.ones((1, npix), jnp.float32)
    design[17 + NBASIS:18 + NBASIS, :] = 2.0 * (cols.astype(jnp.float32) + 0.5) / width - 1.0
    design[18 + NBASIS:19 + NBASIS, :] = 2.0 * (rows.astype(jnp.float32) + 0.5) / height - 1.0

    for copy in tiny_c:
        copy.wait_recv()
    total = s_sum[...]
    for d in range(zn - 1):
        total = total + sc[d]
    denom = 1.0 + total[:, TILES:TILES + 1]
    col_in = lax.broadcasted_iota(jnp.int32, (pr, pcc), 1) + lax.rem(mine, subs) * pcc

    def make_reference(ch, numer):
        scale = jnp.broadcast_to(total[:1, 0:1], (pr, pcc))
        for t in range(1, TILES):
            scale = jnp.where(
                col_in + ch * cw >= t * (width // TILES), jnp.broadcast_to(total[:1, t:t + 1], (pr, pcc)), scale
            )
        return numer / jnp.broadcast_to(denom[:1], (pr, pcc)) * scale

    for ch in range(chunks):
        one.d(ch, make_reference)

    rowi = lax.broadcasted_iota(jnp.int32, (16, LANES), 0)
    lanei = lax.broadcasted_iota(jnp.int32, (16, LANES), 1)
    normal = lax.dot_general(
        design[16:32, :], design[...], (((1,), (1,)), ((), ())),
        precision=lax.Precision.HIGHEST, preferred_element_type=jnp.float32,
    )
    aug = jnp.where(lanei == rowi + 16, normal + 0.05 * normal, normal)
    aug = jnp.where(lanei == rowi, 1.0, aug)
    aug = jnp.where((rowi == 15) & (lanei == 31), 1.0, aug)
    for k in range(NBASIS + 3):
        row = aug[k:k + 1, :] / aug[k:k + 1, 16 + k:17 + k]
        aug = jnp.where(rowi == k, row, aug - aug[:, 16 + k:17 + k] * row)

    for ch in range(chunks):
        one.e(ch)
    for ch in range(chunks):
        one.f(ch)

    picked = jnp.zeros((1, npix), jnp.float32)
    for ch in range(chunks):
        one.h(ch)
        got = jnp.zeros((height, npix), jnp.float32)
        ref_img = jnp.concatenate([group(g1, ch, gi) for gi in range(groups)], axis=0)
        hi = ref_img.astype(jnp.bfloat16)
        rest = ref_img - hi.astype(jnp.float32)
        mid = rest.astype(jnp.bfloat16)
        low = (rest - mid.astype(jnp.float32)).astype(jnp.bfloat16)
        for part in (hi, mid, low):
            got = got + jnp.dot(part, onehot[ch * cw:(ch + 1) * cw, :], preferred_element_type=jnp.float32)
        picked = picked + jnp.sum(jnp.where(row_hit, got, 0.0), axis=0, keepdims=True)
    rhs = jnp.sum(design[16:32, :] * picked, axis=1, keepdims=True)
    coef = jnp.sum(aug * rhs, axis=0, keepdims=True)
    coef_ref[...] = coef[:, 0:NBASIS + 3]

    mask_one = mask[0:1, 0:1]
    span = 16
    xn = 2.0 * (lax.broadcasted_iota(jnp.int32, (1, width), 1).astype(jnp.float32) + 0.5) / width - 1.0
    across_x = coef[:, NBASIS:NBASIS + 1] + coef[:, NBASIS + 1:NBASIS + 2] * xn
    coefs = [coef[:, k:k + 1] for k in range(NBASIS + 3)]
    for ch in range(chunks):
        cols_ch = slice(ch * cw, (ch + 1) * cw)
        for r0 in range(0, height, span):
            model = jnp.zeros((span, cw), jnp.float32)
            for k in range(NBASIS):
                model = model + coefs[k] * bases[k * height + r0:k * height + r0 + span, cols_ch].astype(jnp.float32)
            ynv = (
                2.0 * ((lax.broadcasted_iota(jnp.int32, (span, 1), 0) + r0).astype(jnp.float32) + 0.5) / height - 1.0
            )
            model = model + across_x[:, cols_ch] + coefs[NBASIS + 2] * ynv
            for q in range(span // pr):
                gi = r0 // pr + q
                diff = mask_one * (model[q * pr:(q + 1) * pr, :] - group(g1, ch, gi))
                diff_s[gi * pr:(gi + 1) * pr, cols_ch] = diff
                put_group(x2, ch, gi, diff * diff)
        two.a(ch)
    for ch in range(chunks):
        two.b(ch)
    for ch in range(chunks):
        two.c(ch)
    for ch in range(chunks):
        two.d(ch, lambda ch, pooled: 1.0 / jnp.sqrt(0.05 + pooled / count))
    for ch in range(chunks):
        two.e(ch)
    for ch in range(chunks):
        two.f(ch)
    for ch in range(chunks):
        two.h(ch)
        for gi in range(groups):
            out_ref[0, gi * pr:(gi + 1) * pr, ch * cw:(ch + 1) * cw] = diff_s[
                gi * pr:(gi + 1) * pr, ch * cw:(ch + 1) * cw
            ] * group(g2, ch, gi)
    for copy in pending:
        copy.wait_send()


def shards(images, variance, zero_point, block_mask, stamps, owners):
    _, height, width = images.shape
    count = lax.axis_size("epoch")
    npix = stamps.shape[1]
    zn, yn_count = grid_of(count)
    half = zn * yn_count
    pr = max(8, height // count)
    subs = count * pr // height
    chunks = CHUNKS
    while chunks > 1 and width // chunks // subs < LANES:
        chunks //= 2
    pcc = width // chunks // subs
    f32 = jnp.float32
    big = pltpu.VMEM((chunks, count, pr, pcc), f32)
    ra = pltpu.VMEM((chunks, half, pr, pcc), f32)
    rb = pltpu.VMEM((chunks, max(1, yn_count - 1), zn, pr, pcc), f32)
    rc = pltpu.VMEM((chunks, max(1, zn - 1), pr, pcc), f32)
    tile = pltpu.VMEM((8, LANES), f32)
    nsem = chunks * 2 * (1 + (yn_count - 1) + (zn - 1))
    nsmall = 1 + (yn_count - 1) + (zn - 1)
    dma = pltpu.SemaphoreType.DMA
    vmem = pl.BlockSpec(memory_space=pltpu.VMEM)
    smem = pl.BlockSpec(memory_space=pltpu.SMEM)
    return pl.pallas_call(
        functools.partial(kernel, count, height, width),
        out_shape=(
            jax.ShapeDtypeStruct(images.shape, f32),
            jax.ShapeDtypeStruct((1, NBASIS + 3), f32),
        ),
        in_specs=[vmem, smem, smem, smem, smem, vmem],
        out_specs=(vmem, vmem),
        scratch_shapes=[
            big, big, big, big, ra, ra, rb, rb, rc, rc,
            tile, tile, tile, tile,
            pltpu.VMEM((max(1, yn_count - 1), 8, LANES), f32),
            pltpu.VMEM((max(1, zn - 1), 8, LANES), f32),
            pltpu.VMEM((width // LANES * height, 3 * LANES), jnp.bfloat16),
            pltpu.VMEM((9, height, width), jnp.bfloat16),
            pltpu.VMEM((NBASIS * height, width), jnp.bfloat16),
            pltpu.VMEM((width, npix), jnp.bfloat16),
            pltpu.VMEM((LANES, npix), f32),
            pltpu.VMEM((height, width), f32),
            dma((nsem,)), dma((nsem,)), dma((nsem,)), dma((nsem,)), dma((nsmall,)), dma((nsmall,)),
        ],
        compiler_params=pltpu.CompilerParams(
            collective_id=0, has_side_effects=True, vmem_limit_bytes=56 * 1024 * 1024
        ),
    )(images, variance, zero_point, block_mask, owners, stamps)


def solution(mesh):
    in_specs = (
        P(("patch", "epoch"), None, None),
        P(("patch", "epoch")),
        P(("patch", "epoch")),
        P(("patch", "epoch"), None),
        P(("patch", "epoch"), None),
        P("patch"),
    )
    out_specs = (P(("patch", "epoch"), None, None), P(("patch", "epoch"), None))
    return jax.shard_map(shards, mesh=mesh, in_specs=in_specs, out_specs=out_specs, check_vma=False)
```

```python
import functools
import math

import jax
import jax.numpy as jnp
from jax import lax
from jax.experimental import pallas as pl
from jax.experimental.pallas import tpu as pltpu
from jax.sharding import PartitionSpec as P

TILES = 4
KHALF = 7
NBASIS = 12
LANES = 128

sigma_list = (0.75, 1.5, 3.0)
basis_pairs = ((0, 0), (2, 0), (0, 2), (1, 1))
MESH = pl.DeviceIdType.MESH


def tap_values(offset, sigma, degree):
    scaled = offset / sigma
    power = jnp.ones_like(scaled)
    for _ in range(degree):
        power = power * scaled
    value = jnp.exp(-0.5 * scaled * scaled) * power / (math.sqrt(2.0 * math.pi) * sigma)
    return jnp.where(jnp.abs(offset) <= KHALF, value, 0.0).astype(jnp.bfloat16)


def grid_of(count):
    chips = count // 2
    middle = 1
    while middle * 2 * middle * 2 <= chips:
        middle *= 2
    if chips % middle:
        middle = 1
    return chips // middle, middle


def kernel(
    count, height, width,
    image_ref, var_ref, zp_ref, mask_ref, owner_ref, stamp_ref,
    diff_ref, inv_ref, coef_ref,
    x1, x2, g1, g2, ra1, ra2, rb1, rb2, rc1, rc2,
    s_own, s_mid, s_sum, sa, sb, sc,
    lhs, across, bases, onehot, design,
    send1, recv1, send2, recv2, send3, recv3,
):
    zn, yn_count = grid_of(count)
    half = zn * yn_count
    _, pr, pcc = x1.shape
    subs = width // pcc
    groups = height // pr
    npix = stamp_ref.shape[1]

    me = lax.axis_index("epoch")
    core = lax.rem(me, 2)
    chip = me // 2
    y = lax.rem(chip, yn_count)
    z = chip // yn_count

    def device(zz, yy, cc):
        return {"epoch": (zz * yn_count + yy) * 2 + cc}

    def flip(value, m):
        bit = 1
        while bit <= m:
            if m & bit:
                value = value + bit * (1 - 2 * lax.rem(value // bit, 2))
            bit *= 2
        return value

    mate = device(z, y, 1 - core)
    ys = [flip(y, e) for e in range(1, yn_count)]
    zs = [flip(z, m) for m in range(1, zn)]
    peers = [mate] + [device(z, yy, core) for yy in ys] + [device(zz, y, core) for zz in zs]
    mine = (core * yn_count + y) * zn + z

    barrier = pltpu.get_barrier_semaphore()
    for peer in peers:
        pl.semaphore_signal(barrier, inc=1, device_id=peer, device_id_type=MESH)

    pending = []

    class Lane:
        def __init__(self, send, recv):
            self.send, self.recv, self.next = send, recv, 0

        def start(self, src, dst, device_id):
            copy = pltpu.make_async_remote_copy(
                src_ref=src, dst_ref=dst, send_sem=self.send.at[self.next], recv_sem=self.recv.at[self.next],
                device_id=device_id, device_id_type=MESH,
            )
            self.next += 1
            copy.start()
            pending.append(copy)
            return copy

    order = list(range(zn - 1, -1, -1))

    class Reduce:
        def __init__(self, x, g, ra, rb, rc, lane):
            self.x, self.g, self.ra, self.rb, self.rc, self.lane = x, g, ra, rb, rc, lane
            self.at = {}

        def a(self):
            for m in order:
                zz = flip(z, m)
                for e in list(range(1, yn_count)) + [0]:
                    src = flip(y, e) * zn + zz
                    self.at["a", e, m] = self.lane.start(
                        self.x.at[(1 - core) * half + src], self.ra.at[src], mate
                    )

        def b(self, m):
            zz = flip(z, m)
            for e in range(1, yn_count):
                yy = flip(y, e)
                own = core * half + yy * zn + zz
                self.at["a", e, m].wait_recv()
                self.x[own] = self.x[own] + self.ra[yy * zn + zz]
                self.at["b", e, m] = self.lane.start(self.x.at[own], self.rb.at[e - 1, zz], device(z, yy, core))

        def c(self, m):
            zz = flip(z, m)
            own = core * half + y * zn + zz
            self.at["a", 0, m].wait_recv()
            total = self.x[own] + self.ra[y * zn + zz]
            for e in range(1, yn_count):
                self.at["b", e, m].wait_recv()
                total = total + self.rb[e - 1, zz]
            self.x[own] = total
            if m:
                self.at["c", m] = self.lane.start(self.x.at[own], self.rc.at[m - 1], device(zz, y, core))

        def d(self, final):
            total = self.x[mine]
            for m in order[::-1]:
                if m:
                    self.at["c", m].wait_recv()
                    total = total + self.rc[m - 1]
            self.g[mine] = final(total)
            for m in order:
                if m:
                    self.at["d", m] = self.lane.start(
                        self.g.at[mine], self.g.at[mine], device(flip(z, m), y, core)
                    )
            self.forward(0)

        def forward(self, m):
            if m:
                self.at["d", m].wait_recv()
            block = self.g.at[(core * yn_count + y) * zn + flip(z, m)]
            for e in range(1, yn_count):
                self.at["e", e, m] = self.lane.start(block, block, device(z, flip(y, e), core))
            self.at["f", 0, m] = self.lane.start(block, block, mate)

        def mate_on(self, m):
            for e in range(1, yn_count):
                self.at["e", e, m].wait_recv()
                block = self.g.at[(core * yn_count + flip(y, e)) * zn + flip(z, m)]
                self.at["f", e, m] = self.lane.start(block, block, mate)

        def end(self):
            for m in order[::-1]:
                for e in range(yn_count):
                    self.at["f", e, m].wait_recv()

    def group(ref, gi):
        parts = [ref[gi * subs + s] for s in range(subs)]
        return parts[0] if subs == 1 else jnp.concatenate(parts, axis=1)

    def put_group(ref, gi, value):
        for s in range(subs):
            ref[gi * subs + s] = value[:, s * pcc:(s + 1) * pcc]

    one = Reduce(x1, g1, ra1, rb1, rc1, Lane(send1, recv1))
    two = Reduce(x2, g2, ra2, rb2, rc2, Lane(send2, recv2))
    tiny = Lane(send3, recv3)

    weight = 1.0 / jnp.broadcast_to(var_ref[...], (8, LANES))
    mask = jnp.broadcast_to(mask_ref[...].astype(jnp.float32), (8, LANES))
    block_term = weight * mask
    term = block_term[0:1, 0:1]
    lane = lax.broadcasted_iota(jnp.int32, (8, LANES), 1)
    small = jnp.where(lane == TILES, block_term, 0.0)
    for t in range(TILES):
        owned = jnp.broadcast_to(owner_ref[:, t:t + 1], (8, LANES)) == me
        small = small + jnp.where((lane == t) & owned, jnp.broadcast_to(zp_ref[...], (8, LANES)), 0.0)
    s_own[...] = small
    for gi in range(groups):
        put_group(x1, gi, image_ref[0, gi * pr:(gi + 1) * pr, :] * term)

    pl.semaphore_wait(barrier, len(peers))
    tiny_a = [tiny.start(s_own, sa, mate)]
    one.a()

    sharp = image_ref[0].astype(jnp.bfloat16)
    ntile = width // LANES
    zero = jnp.zeros((height, LANES), jnp.bfloat16)
    for t in range(ntile):
        for s in range(3):
            src = t + s - 1
            value = sharp[:, src * LANES:(src + 1) * LANES] if 0 <= src < ntile else zero
            lhs[t * height:(t + 1) * height, s * LANES:(s + 1) * LANES] = value
    off_h = (
        lax.broadcasted_iota(jnp.int32, (3 * LANES, LANES), 0)
        - LANES
        - lax.broadcasted_iota(jnp.int32, (3 * LANES, LANES), 1)
    ).astype(jnp.float32)
    off_v = (
        lax.broadcasted_iota(jnp.int32, (height, height), 1) - lax.broadcasted_iota(jnp.int32, (height, height), 0)
    ).astype(jnp.float32)

    def horizontal(si):
        sigma = sigma_list[si]
        band = jnp.concatenate([tap_values(off_h, sigma, degree) for degree in (0, 1, 2)], axis=1)
        for t in range(0, ntile, 2):
            res = jnp.dot(
                lhs[t * height:(t + 2) * height, :], band, preferred_element_type=jnp.float32
            ).astype(jnp.bfloat16)
            for u in range(2):
                for degree in (0, 1, 2):
                    across[si * 3 + degree, :, (t + u) * LANES:(t + u + 1) * LANES] = res[
                        u * height:(u + 1) * height, degree * LANES:(degree + 1) * LANES
                    ]

    def vertical(si):
        sigma = sigma_list[si]
        bands = [tap_values(off_v, sigma, degree) for degree in (0, 1, 2)]
        for i, j in basis_pairs:
            k = si * 4 + basis_pairs.index((i, j))
            bases[k * height:(k + 1) * height, :] = jnp.dot(
                bands[j], across[si * 3 + i], preferred_element_type=jnp.float32
            ).astype(jnp.bfloat16)

    horizontal(0)

    tiny_a[0].wait_recv()
    s_mid[...] = s_own[...] + sa[...]
    tiny_b = [tiny.start(s_mid, sb.at[d], device(z, yy, core)) for d, yy in enumerate(ys)]
    for m in order:
        one.b(m)

    horizontal(1)

    for copy in tiny_b:
        copy.wait_recv()
    total = s_mid[...]
    for d in range(yn_count - 1):
        total = total + sb[d]
    s_sum[...] = total
    tiny_c = [tiny.start(s_sum, sc.at[d], device(zz, y, core)) for d, zz in enumerate(zs)]
    for m in order:
        one.c(m)
    horizontal(2)
    for si in range(3):
        vertical(si)

    stamp = stamp_ref[...]
    shift = width.bit_length() - 1
    rows = lax.shift_right_logical(stamp, shift)
    cols = stamp - lax.shift_left(rows, shift)
    onehot[...] = jnp.where(
        lax.broadcasted_iota(jnp.int32, (width, npix), 0) == cols, 1.0, 0.0
    ).astype(jnp.bfloat16)
    row_hit = lax.broadcasted_iota(jnp.int32, (height, npix), 0) == rows
    design[...] = jnp.zeros_like(design)

    def pick(k):
        got = jnp.dot(
            bases[k * height:(k + 1) * height, :], onehot[...], preferred_element_type=jnp.float32
        )
        design[16 + k:17 + k, :] = jnp.sum(jnp.where(row_hit, got, 0.0), axis=0, keepdims=True)

    design[16 + NBASIS:17 + NBASIS, :] = jnp.ones((1, npix), jnp.float32)
    design[17 + NBASIS:18 + NBASIS, :] = 2.0 * (cols.astype(jnp.float32) + 0.5) / width - 1.0
    design[18 + NBASIS:19 + NBASIS, :] = 2.0 * (rows.astype(jnp.float32) + 0.5) / height - 1.0

    for copy in tiny_c:
        copy.wait_recv()
    total = s_sum[...]
    for d in range(zn - 1):
        total = total + sc[d]
    denom = 1.0 + total[:, TILES:TILES + 1]
    col_in = lax.broadcasted_iota(jnp.int32, (pr, pcc), 1) + lax.rem(mine, subs) * pcc

    def make_reference(numer):
        scale = jnp.broadcast_to(total[:1, 0:1], (pr, pcc))
        for t in range(1, TILES):
            scale = jnp.where(
                col_in >= t * (width // TILES), jnp.broadcast_to(total[:1, t:t + 1], (pr, pcc)), scale
            )
        return numer / jnp.broadcast_to(denom[:1], (pr, pcc)) * scale

    one.d(make_reference)
    for k in range(NBASIS // 2):
        pick(k)
    for m in range(1, zn):
        one.forward(m)
    for k in range(NBASIS // 2, NBASIS):
        pick(k)
    for m in range(zn):
        one.mate_on(m)

    rowi = lax.broadcasted_iota(jnp.int32, (16, LANES), 0)
    lanei = lax.broadcasted_iota(jnp.int32, (16, LANES), 1)
    normal = lax.dot_general(
        design[16:32, :], design[...], (((1,), (1,)), ((), ())),
        precision=lax.Precision.HIGHEST, preferred_element_type=jnp.float32,
    )
    aug = jnp.where(lanei == rowi + 16, normal + 0.05 * normal, normal)
    aug = jnp.where(lanei == rowi, 1.0, aug)
    aug = jnp.where((rowi == 15) & (lanei == 31), 1.0, aug)
    for k in range(NBASIS + 3):
        row = aug[k:k + 1, :] / aug[k:k + 1, 16 + k:17 + k]
        aug = jnp.where(rowi == k, row, aug - aug[:, 16 + k:17 + k] * row)

    one.end()
    ref_img = jnp.concatenate([group(g1, gi) for gi in range(groups)], axis=0)
    hi = ref_img.astype(jnp.bfloat16)
    rest = ref_img - hi.astype(jnp.float32)
    mid = rest.astype(jnp.bfloat16)
    low = (rest - mid.astype(jnp.float32)).astype(jnp.bfloat16)
    got = jnp.zeros((height, npix), jnp.float32)
    for part in (hi, mid, low):
        got = got + jnp.dot(part, onehot[...], preferred_element_type=jnp.float32)
    picked = jnp.sum(jnp.where(row_hit, got, 0.0), axis=0, keepdims=True)
    rhs = jnp.sum(design[16:32, :] * picked, axis=1, keepdims=True)
    coef = jnp.sum(aug * rhs, axis=0, keepdims=True)
    coef_ref[...] = coef[:, 0:NBASIS + 3]

    mask_one = mask[0:1, 0:1]
    span = 16
    xn = 2.0 * (lax.broadcasted_iota(jnp.int32, (1, width), 1).astype(jnp.float32) + 0.5) / width - 1.0
    across_x = coef[:, NBASIS:NBASIS + 1] + coef[:, NBASIS + 1:NBASIS + 2] * xn
    coefs = [coef[:, k:k + 1] for k in range(NBASIS + 3)]
    for r0 in range(0, height, span):
        model = jnp.zeros((span, width), jnp.float32)
        for k in range(NBASIS):
            model = model + coefs[k] * bases[k * height + r0:k * height + r0 + span, :].astype(jnp.float32)
        ynv = 2.0 * ((lax.broadcasted_iota(jnp.int32, (span, 1), 0) + r0).astype(jnp.float32) + 0.5) / height - 1.0
        model = model + across_x + coefs[NBASIS + 2] * ynv
        for q in range(span // pr):
            gi = r0 // pr + q
            diff = mask_one * (model[q * pr:(q + 1) * pr, :] - group(g1, gi))
            diff_ref[gi * pr:(gi + 1) * pr, :] = diff
            put_group(x2, gi, diff * diff)
    two.a()
    for m in order:
        two.b(m)
    for m in order:
        two.c(m)
    two.d(lambda pooled: 1.0 / jnp.sqrt(0.05 + pooled / count))
    for m in range(1, zn):
        two.forward(m)
    for m in range(zn):
        two.mate_on(m)
    two.end()
    for gi in range(groups):
        inv_ref[gi * pr:(gi + 1) * pr, :] = group(g2, gi)
    for copy in pending:
        copy.wait_send()


def finish(diff_ref, inv_ref, coef_in, out_ref, coef_ref):
    out_ref[0] = diff_ref[...] * inv_ref[...]
    coef_ref[...] = coef_in[...]


def shards(images, variance, zero_point, block_mask, stamps, owners):
    _, height, width = images.shape
    count = lax.axis_size("epoch")
    npix = stamps.shape[1]
    zn, yn_count = grid_of(count)
    half = zn * yn_count
    pr = max(8, height // count)
    subs = count * pr // height
    pcc = width // subs
    f32 = jnp.float32
    big = pltpu.VMEM((count, pr, pcc), f32)
    ra = pltpu.VMEM((half, pr, pcc), f32)
    rb = pltpu.VMEM((max(1, yn_count - 1), zn, pr, pcc), f32)
    rc = pltpu.VMEM((max(1, zn - 1), pr, pcc), f32)
    tile = pltpu.VMEM((8, LANES), f32)
    nsem = 2 * (half + (yn_count - 1) * zn + (zn - 1))
    nsmall = 1 + (yn_count - 1) + (zn - 1)
    dma = pltpu.SemaphoreType.DMA
    vmem = pl.BlockSpec(memory_space=pltpu.VMEM)
    diff, inv, coef = pl.pallas_call(
        functools.partial(kernel, count, height, width),
        out_shape=(
            jax.ShapeDtypeStruct((height, width), f32),
            jax.ShapeDtypeStruct((height, width), f32),
            jax.ShapeDtypeStruct((1, NBASIS + 3), f32),
        ),
        in_specs=[vmem] * 6,
        out_specs=(vmem,) * 3,
        scratch_shapes=[
            big, big, big, big, ra, ra, rb, rb, rc, rc,
            tile, tile, tile, tile,
            pltpu.VMEM((max(1, yn_count - 1), 8, LANES), f32),
            pltpu.VMEM((max(1, zn - 1), 8, LANES), f32),
            pltpu.VMEM((width // LANES * height, 3 * LANES), jnp.bfloat16),
            pltpu.VMEM((9, height, width), jnp.bfloat16),
            pltpu.VMEM((NBASIS * height, width), jnp.bfloat16),
            pltpu.VMEM((width, npix), jnp.bfloat16),
            pltpu.VMEM((LANES, npix), f32),
            dma((nsem,)), dma((nsem,)), dma((nsem,)), dma((nsem,)), dma((nsmall,)), dma((nsmall,)),
        ],
        compiler_params=pltpu.CompilerParams(
            collective_id=0, has_side_effects=True, vmem_limit_bytes=40 * 1024 * 1024
        ),
    )(
        images, variance.reshape(1, 1), zero_point.reshape(1, 1), block_mask, owners.reshape(1, -1), stamps
    )
    return pl.pallas_call(
        finish,
        out_shape=(
            jax.ShapeDtypeStruct(images.shape, f32),
            jax.ShapeDtypeStruct((1, NBASIS + 3), f32),
        ),
        in_specs=[vmem] * 3,
        out_specs=(vmem,) * 2,
        compiler_params=pltpu.CompilerParams(vmem_limit_bytes=8 * 1024 * 1024),
    )(diff, inv, coef)


def solution(mesh):
    in_specs = (
        P(("patch", "epoch"), None, None),
        P(("patch", "epoch")),
        P(("patch", "epoch")),
        P(("patch", "epoch"), None),
        P(("patch", "epoch"), None),
        P("patch"),
    )
    out_specs = (P(("patch", "epoch"), None, None), P(("patch", "epoch"), None))
    return jax.shard_map(shards, mesh=mesh, in_specs=in_specs, out_specs=out_specs, check_vma=False)
```

```python
import functools
import math

import jax
import jax.numpy as jnp
from jax import lax
from jax.experimental import pallas as pl
from jax.experimental.pallas import tpu as pltpu
from jax.sharding import PartitionSpec as P

TILES = 4
KHALF = 7
NBASIS = 12
LANES = 128

sigma_list = (0.75, 1.5, 3.0)
basis_pairs = ((0, 0), (2, 0), (0, 2), (1, 1))
MESH = pl.DeviceIdType.MESH


def tap_values(offset, sigma, degree):
    scaled = offset / sigma
    power = jnp.ones_like(scaled)
    for _ in range(degree):
        power = power * scaled
    value = jnp.exp(-0.5 * scaled * scaled) * power / (math.sqrt(2.0 * math.pi) * sigma)
    return jnp.where(jnp.abs(offset) <= KHALF, value, 0.0).astype(jnp.bfloat16)


def grid_of(count):
    chips = count // 2
    middle = 1
    while middle * 2 * middle * 2 <= chips:
        middle *= 2
    if chips % middle:
        middle = 1
    return chips // middle, middle


def kernel(
    count, height, width,
    image_in, var_in, zp_in, mask_in, owner_in, stamp_in,
    diff_ref, inv_ref, coef_ref,
    x1, x2, g1, g2, ra1, ra2, rb1, rb2, rc1, rc2,
    s_own, s_mid, s_sum, sa, sb, sc,
    lhs, across, bases, onehot, design,
    image_ref, var_ref, zp_ref, mask_ref, owner_ref, stamp_ref, load,
    send1, recv1, send2, recv2, send3, recv3,
):
    zn, yn_count = grid_of(count)
    half = zn * yn_count
    _, pr, pcc = x1.shape
    subs = width // pcc
    groups = height // pr
    npix = stamp_ref.shape[1]

    me = lax.axis_index("epoch")
    core = lax.rem(me, 2)
    chip = me // 2
    y = lax.rem(chip, yn_count)
    z = chip // yn_count

    def device(zz, yy, cc):
        return {"epoch": (zz * yn_count + yy) * 2 + cc}

    def flip(value, m):
        bit = 1
        while bit <= m:
            if m & bit:
                value = value + bit * (1 - 2 * lax.rem(value // bit, 2))
            bit *= 2
        return value

    mate = device(z, y, 1 - core)
    ys = [flip(y, e) for e in range(1, yn_count)]
    zs = [flip(z, m) for m in range(1, zn)]
    peers = [mate] + [device(z, yy, core) for yy in ys] + [device(zz, y, core) for zz in zs]
    mine = (core * yn_count + y) * zn + z

    barrier = pltpu.get_barrier_semaphore()
    for peer in peers:
        pl.semaphore_signal(barrier, inc=1, device_id=peer, device_id_type=MESH)

    loads = [
        pltpu.make_async_copy(src, dst, load.at[i])
        for i, (src, dst) in enumerate((
            (image_in, image_ref), (var_in, var_ref), (mask_in, mask_ref),
            (zp_in, zp_ref), (owner_in, owner_ref), (stamp_in, stamp_ref),
        ))
    ]
    for copy in loads:
        copy.start()

    pending = []

    class Lane:
        def __init__(self, send, recv):
            self.send, self.recv, self.next = send, recv, 0

        def start(self, src, dst, device_id):
            copy = pltpu.make_async_remote_copy(
                src_ref=src, dst_ref=dst, send_sem=self.send.at[self.next], recv_sem=self.recv.at[self.next],
                device_id=device_id, device_id_type=MESH,
            )
            self.next += 1
            copy.start()
            pending.append(copy)
            return copy

    order = list(range(zn - 1, -1, -1))

    class Reduce:
        def __init__(self, x, g, ra, rb, rc, lane):
            self.x, self.g, self.ra, self.rb, self.rc, self.lane = x, g, ra, rb, rc, lane
            self.at = {}

        def a(self):
            for m in order:
                zz = flip(z, m)
                for e in list(range(1, yn_count)) + [0]:
                    src = flip(y, e) * zn + zz
                    self.at["a", e, m] = self.lane.start(
                        self.x.at[(1 - core) * half + src], self.ra.at[src], mate
                    )

        def b(self, m):
            zz = flip(z, m)
            for e in range(1, yn_count):
                yy = flip(y, e)
                own = core * half + yy * zn + zz
                self.at["a", e, m].wait_recv()
                self.x[own] = self.x[own] + self.ra[yy * zn + zz]
                self.at["b", e, m] = self.lane.start(self.x.at[own], self.rb.at[e - 1, zz], device(z, yy, core))

        def c(self, m):
            zz = flip(z, m)
            own = core * half + y * zn + zz
            self.at["a", 0, m].wait_recv()
            total = self.x[own] + self.ra[y * zn + zz]
            for e in range(1, yn_count):
                self.at["b", e, m].wait_recv()
                total = total + self.rb[e - 1, zz]
            self.x[own] = total
            if m:
                self.at["c", m] = self.lane.start(self.x.at[own], self.rc.at[m - 1], device(zz, y, core))

        def d(self, final):
            total = self.x[mine]
            for m in order[::-1]:
                if m:
                    self.at["c", m].wait_recv()
                    total = total + self.rc[m - 1]
            self.g[mine] = final(total)
            for m in order:
                if m:
                    self.at["d", m] = self.lane.start(
                        self.g.at[mine], self.g.at[mine], device(flip(z, m), y, core)
                    )
            self.forward(0)

        def forward(self, m):
            if m:
                self.at["d", m].wait_recv()
            block = self.g.at[(core * yn_count + y) * zn + flip(z, m)]
            for e in range(1, yn_count):
                self.at["e", e, m] = self.lane.start(block, block, device(z, flip(y, e), core))
            self.at["f", 0, m] = self.lane.start(block, block, mate)

        def mate_on(self, m):
            for e in range(1, yn_count):
                self.at["e", e, m].wait_recv()
                block = self.g.at[(core * yn_count + flip(y, e)) * zn + flip(z, m)]
                self.at["f", e, m] = self.lane.start(block, block, mate)

        def end(self):
            for m in order[::-1]:
                for e in range(yn_count):
                    self.at["f", e, m].wait_recv()

    def group(ref, gi):
        parts = [ref[gi * subs + s] for s in range(subs)]
        return parts[0] if subs == 1 else jnp.concatenate(parts, axis=1)

    def put_group(ref, gi, value):
        for s in range(subs):
            ref[gi * subs + s] = value[:, s * pcc:(s + 1) * pcc]

    one = Reduce(x1, g1, ra1, rb1, rc1, Lane(send1, recv1))
    two = Reduce(x2, g2, ra2, rb2, rc2, Lane(send2, recv2))
    tiny = Lane(send3, recv3)

    for copy in loads:
        copy.wait()
    weight = 1.0 / jnp.full((8, LANES), var_ref[0], jnp.float32)
    mask = jnp.full((8, LANES), mask_ref[0, 0].astype(jnp.float32), jnp.float32)
    block_term = weight * mask
    term = block_term[0:1, 0:1]
    lane = lax.broadcasted_iota(jnp.int32, (8, LANES), 1)
    small = jnp.where(lane == TILES, block_term, 0.0)
    for t in range(TILES):
        value = jnp.where(owner_ref[t] == me, zp_ref[0], 0.0)
        small = small + jnp.where(lane == t, value, 0.0)
    s_own[...] = small
    for gi in range(groups):
        put_group(x1, gi, image_ref[0, gi * pr:(gi + 1) * pr, :] * term)

    pl.semaphore_wait(barrier, len(peers))
    tiny_a = [tiny.start(s_own, sa, mate)]
    one.a()

    sharp = image_ref[0].astype(jnp.bfloat16)
    ntile = width // LANES
    zero = jnp.zeros((height, LANES), jnp.bfloat16)
    for t in range(ntile):
        for s in range(3):
            src = t + s - 1
            value = sharp[:, src * LANES:(src + 1) * LANES] if 0 <= src < ntile else zero
            lhs[t * height:(t + 1) * height, s * LANES:(s + 1) * LANES] = value
    off_h = (
        lax.broadcasted_iota(jnp.int32, (3 * LANES, LANES), 0)
        - LANES
        - lax.broadcasted_iota(jnp.int32, (3 * LANES, LANES), 1)
    ).astype(jnp.float32)
    off_v = (
        lax.broadcasted_iota(jnp.int32, (height, height), 1) - lax.broadcasted_iota(jnp.int32, (height, height), 0)
    ).astype(jnp.float32)

    def horizontal(si):
        sigma = sigma_list[si]
        band = jnp.concatenate([tap_values(off_h, sigma, degree) for degree in (0, 1, 2)], axis=1)
        for t in range(0, ntile, 2):
            res = jnp.dot(
                lhs[t * height:(t + 2) * height, :], band, preferred_element_type=jnp.float32
            ).astype(jnp.bfloat16)
            for u in range(2):
                for degree in (0, 1, 2):
                    across[si * 3 + degree, :, (t + u) * LANES:(t + u + 1) * LANES] = res[
                        u * height:(u + 1) * height, degree * LANES:(degree + 1) * LANES
                    ]

    def vertical(si):
        sigma = sigma_list[si]
        bands = [tap_values(off_v, sigma, degree) for degree in (0, 1, 2)]
        for i, j in basis_pairs:
            k = si * 4 + basis_pairs.index((i, j))
            bases[k * height:(k + 1) * height, :] = jnp.dot(
                bands[j], across[si * 3 + i], preferred_element_type=jnp.float32
            ).astype(jnp.bfloat16)

    horizontal(0)

    tiny_a[0].wait_recv()
    s_mid[...] = s_own[...] + sa[...]
    tiny_b = [tiny.start(s_mid, sb.at[d], device(z, yy, core)) for d, yy in enumerate(ys)]
    for m in order:
        one.b(m)

    horizontal(1)

    for copy in tiny_b:
        copy.wait_recv()
    total = s_mid[...]
    for d in range(yn_count - 1):
        total = total + sb[d]
    s_sum[...] = total
    tiny_c = [tiny.start(s_sum, sc.at[d], device(zz, y, core)) for d, zz in enumerate(zs)]
    for m in order:
        one.c(m)
    horizontal(2)
    for si in range(3):
        vertical(si)

    stamp = stamp_ref[...]
    shift = width.bit_length() - 1
    rows = lax.shift_right_logical(stamp, shift)
    cols = stamp - lax.shift_left(rows, shift)
    onehot[...] = jnp.where(
        lax.broadcasted_iota(jnp.int32, (width, npix), 0) == cols, 1.0, 0.0
    ).astype(jnp.bfloat16)
    row_hit = lax.broadcasted_iota(jnp.int32, (height, npix), 0) == rows
    design[...] = jnp.zeros_like(design)

    def pick(k):
        got = jnp.dot(
            bases[k * height:(k + 1) * height, :], onehot[...], preferred_element_type=jnp.float32
        )
        design[16 + k:17 + k, :] = jnp.sum(jnp.where(row_hit, got, 0.0), axis=0, keepdims=True)

    design[16 + NBASIS:17 + NBASIS, :] = jnp.ones((1, npix), jnp.float32)
    design[17 + NBASIS:18 + NBASIS, :] = 2.0 * (cols.astype(jnp.float32) + 0.5) / width - 1.0
    design[18 + NBASIS:19 + NBASIS, :] = 2.0 * (rows.astype(jnp.float32) + 0.5) / height - 1.0

    for copy in tiny_c:
        copy.wait_recv()
    total = s_sum[...]
    for d in range(zn - 1):
        total = total + sc[d]
    denom = 1.0 + total[:, TILES:TILES + 1]
    col_in = lax.broadcasted_iota(jnp.int32, (pr, pcc), 1) + lax.rem(mine, subs) * pcc

    def make_reference(numer):
        scale = jnp.broadcast_to(total[:1, 0:1], (pr, pcc))
        for t in range(1, TILES):
            scale = jnp.where(
                col_in >= t * (width // TILES), jnp.broadcast_to(total[:1, t:t + 1], (pr, pcc)), scale
            )
        return numer / jnp.broadcast_to(denom[:1], (pr, pcc)) * scale

    one.d(make_reference)
    for k in range(NBASIS // 2):
        pick(k)
    for m in range(1, zn):
        one.forward(m)
    for k in range(NBASIS // 2, NBASIS):
        pick(k)
    for m in range(zn):
        one.mate_on(m)

    rowi = lax.broadcasted_iota(jnp.int32, (16, LANES), 0)
    lanei = lax.broadcasted_iota(jnp.int32, (16, LANES), 1)
    normal = lax.dot_general(
        design[16:32, :], design[...], (((1,), (1,)), ((), ())),
        precision=lax.Precision.HIGHEST, preferred_element_type=jnp.float32,
    )
    aug = jnp.where(lanei == rowi + 16, normal + 0.05 * normal, normal)
    aug = jnp.where(lanei == rowi, 1.0, aug)
    aug = jnp.where((rowi == 15) & (lanei == 31), 1.0, aug)
    for k in range(NBASIS + 3):
        row = aug[k:k + 1, :] / aug[k:k + 1, 16 + k:17 + k]
        aug = jnp.where(rowi == k, row, aug - aug[:, 16 + k:17 + k] * row)

    mid_row = height // 2
    half_row = lax.broadcasted_iota(jnp.int32, (mid_row, npix), 0)

    def picked_of(side):
        ref_img = jnp.concatenate([group(g1, side * (groups // 2) + gi) for gi in range(groups // 2)], axis=0)
        hi = ref_img.astype(jnp.bfloat16)
        rest = ref_img - hi.astype(jnp.float32)
        mid = rest.astype(jnp.bfloat16)
        low = (rest - mid.astype(jnp.float32)).astype(jnp.bfloat16)
        got = jnp.zeros((mid_row, npix), jnp.float32)
        for part in (hi, mid, low):
            got = got + jnp.dot(part, onehot[...], preferred_element_type=jnp.float32)
        return jnp.sum(jnp.where(half_row + side * mid_row == rows, got, 0.0), axis=0, keepdims=True)

    picked = picked_of(core)
    one.end()
    picked = picked + picked_of(1 - core)
    rhs = jnp.sum(design[16:32, :] * picked, axis=1, keepdims=True)
    coef = jnp.sum(aug * rhs, axis=0, keepdims=True)
    coef_ref[...] = coef[:, 0:NBASIS + 3]

    mask_one = mask[0:1, 0:1]
    span = 16
    xn = 2.0 * (lax.broadcasted_iota(jnp.int32, (1, width), 1).astype(jnp.float32) + 0.5) / width - 1.0
    across_x = coef[:, NBASIS:NBASIS + 1] + coef[:, NBASIS + 1:NBASIS + 2] * xn
    coefs = [coef[:, k:k + 1] for k in range(NBASIS + 3)]
    for r0 in range(0, height, span):
        side = 1 - core if r0 < mid_row else core
        if r0 == mid_row:
            two.a()
        row = pl.multiple_of(side * mid_row + r0 % mid_row, span)
        model = jnp.zeros((span, width), jnp.float32)
        for k in range(NBASIS):
            model = model + coefs[k] * bases[pl.ds(k * height + row, span), :].astype(jnp.float32)
        ynv = 2.0 * ((lax.broadcasted_iota(jnp.int32, (span, 1), 0) + row).astype(jnp.float32) + 0.5) / height - 1.0
        model = model + across_x + coefs[NBASIS + 2] * ynv
        for q in range(span // pr):
            gi = row // pr + q
            diff = mask_one * (model[q * pr:(q + 1) * pr, :] - group(g1, gi))
            diff_ref[pl.ds(pl.multiple_of(row + q * pr, pr), pr), :] = diff
            put_group(x2, gi, diff * diff)
    for m in order:
        two.b(m)
    for m in order:
        two.c(m)
    two.d(lambda pooled: 1.0 / jnp.sqrt(0.05 + pooled / count))
    for m in range(1, zn):
        two.forward(m)
    for m in range(zn):
        two.mate_on(m)
    two.end()
    for gi in range(groups):
        inv_ref[gi * pr:(gi + 1) * pr, :] = group(g2, gi)
    for copy in pending:
        copy.wait_send()


def finish(diff_ref, inv_ref, coef_in, out_ref, coef_ref):
    out_ref[0] = diff_ref[...] * inv_ref[...]
    coef_ref[...] = coef_in[...]


def shards(images, variance, zero_point, block_mask, stamps, owners):
    _, height, width = images.shape
    count = lax.axis_size("epoch")
    npix = stamps.shape[1]
    zn, yn_count = grid_of(count)
    half = zn * yn_count
    pr = max(8, height // count)
    subs = count * pr // height
    pcc = width // subs
    f32 = jnp.float32
    big = pltpu.VMEM((count, pr, pcc), f32)
    ra = pltpu.VMEM((half, pr, pcc), f32)
    rb = pltpu.VMEM((max(1, yn_count - 1), zn, pr, pcc), f32)
    rc = pltpu.VMEM((max(1, zn - 1), pr, pcc), f32)
    tile = pltpu.VMEM((8, LANES), f32)
    nsem = 2 * (half + (yn_count - 1) * zn + (zn - 1))
    nsmall = 1 + (yn_count - 1) + (zn - 1)
    dma = pltpu.SemaphoreType.DMA
    vmem = pl.BlockSpec(memory_space=pltpu.VMEM)
    diff, inv, coef = pl.pallas_call(
        functools.partial(kernel, count, height, width),
        out_shape=(
            jax.ShapeDtypeStruct((height, width), f32),
            jax.ShapeDtypeStruct((height, width), f32),
            jax.ShapeDtypeStruct((1, NBASIS + 3), f32),
        ),
        in_specs=[pl.BlockSpec(memory_space=pltpu.HBM)] * 6,
        out_specs=(vmem,) * 3,
        scratch_shapes=[
            big, big, big, big, ra, ra, rb, rb, rc, rc,
            tile, tile, tile, tile,
            pltpu.VMEM((max(1, yn_count - 1), 8, LANES), f32),
            pltpu.VMEM((max(1, zn - 1), 8, LANES), f32),
            pltpu.VMEM((width // LANES * height, 3 * LANES), jnp.bfloat16),
            pltpu.VMEM((9, height, width), jnp.bfloat16),
            pltpu.VMEM((NBASIS * height, width), jnp.bfloat16),
            pltpu.VMEM((width, npix), jnp.bfloat16),
            pltpu.VMEM((LANES, npix), f32),
            pltpu.VMEM(images.shape, f32),
            pltpu.SMEM((1,), f32), pltpu.SMEM((1,), f32),
            pltpu.SMEM(block_mask.shape, jnp.int32), pltpu.SMEM(owners.shape, jnp.int32),
            pltpu.VMEM(stamps.shape, jnp.int32), dma((6,)),
            dma((nsem,)), dma((nsem,)), dma((nsem,)), dma((nsem,)), dma((nsmall,)), dma((nsmall,)),
        ],
        compiler_params=pltpu.CompilerParams(
            collective_id=0, has_side_effects=True, vmem_limit_bytes=40 * 1024 * 1024
        ),
    )(images, variance, zero_point, block_mask, owners, stamps)
    return pl.pallas_call(
        finish,
        out_shape=(
            jax.ShapeDtypeStruct(images.shape, f32),
            jax.ShapeDtypeStruct((1, NBASIS + 3), f32),
        ),
        in_specs=[vmem] * 3,
        out_specs=(vmem,) * 2,
        compiler_params=pltpu.CompilerParams(vmem_limit_bytes=8 * 1024 * 1024),
    )(diff, inv, coef)


def solution(mesh):
    in_specs = (
        P(("patch", "epoch"), None, None),
        P(("patch", "epoch")),
        P(("patch", "epoch")),
        P(("patch", "epoch"), None),
        P(("patch", "epoch"), None),
        P("patch"),
    )
    out_specs = (P(("patch", "epoch"), None, None), P(("patch", "epoch"), None))
    return jax.shard_map(shards, mesh=mesh, in_specs=in_specs, out_specs=out_specs, check_vma=False)
```
